256 devices in a mesh: aper: 64 (over z_hi, y, x), shot: 4 (over z_lo, core).
Axes of the slice: x: 4, y: 4, z: 8 (z_hi: 4, z_lo: 2; z = z_hi * 2 + z_lo), core: 2. Of those that a mesh axis runs over, the one named last changes fastest.
Arguments:
- wavefield: float32 [4, 9, 256, 128, 128], P('shot', None, 'aper'), may hold values from -6 to 6
- lame_lambda: float32 [256, 128, 128], P('aper', 'shot'), may hold values from 0.5 to 2
- lame_mu: float32 [256, 128, 128], P('aper', 'shot'), may hold values from 0.3 to 1
- buoyancy: float32 [256, 128, 128], P('aper', 'shot'), may hold values from 0.4 to 1
- quality: float32 [256, 128, 128], P('aper', 'shot'), may hold values from 0.05 to 2
- active: int32 [4, 64, 4, 4], replicated, may hold values 0 or 1
Outputs:
- final_field: float32 [4, 9, 256, 128, 128], P('shot', None, 'aper')
The draws below stay inside these ranges and needn't reach their ends.
All inputs are finite; a program needn't handle non-finite values.
Results may differ from the reference program's by a relative error of at most 0.00002.
Values sent between devices are 32-bit elements; how exact they have to be, the bound alone decides.
A program may use at most 64 MiB of HBM per device.

```python
import math
import jax
import jax.numpy as jnp
from jax import lax

CX = 4
NY = 128
NZ = 128
BLK = 32
STEPS = 4
SHOTS = 4
NX = 256
NBY = 4
NBZ = 4
N_APER = 64


def with_ends(array, key, smallest, largest):
    longest = array.shape.index(max(array.shape))
    spots = []
    for shift in (0, 1):
        where = [jax.random.randint(jax.random.fold_in(key, axis), (), 0, length) for axis, length in enumerate(array.shape)]
        where[longest] = (where[longest] + shift) % array.shape[longest]
        spots.append(tuple(where))
    return array.at[spots[0]].set(smallest).at[spots[1]].set(largest)


def block_scale(rng, extent, pieces, least, largest):
    level, own = 1.0, jax.random.fold_in(rng, 6)
    for axis_at, blocks in pieces:
        draws = jnp.exp(jax.random.uniform(jax.random.fold_in(own, axis_at), (blocks,), jnp.float32, least / len(pieces), largest / len(pieces)))
        level = level * jnp.repeat(draws, extent[axis_at] // blocks).reshape([-1 if axis == axis_at else 1 for axis in range(len(extent))])
    return level


def normal_values(key, dims, scale, reach, shards=(), held_as=jnp.bfloat16):
    entries = scale * jax.random.normal(key, dims, jnp.float32)
    if shards:
        entries = entries * block_scale(key, dims, shards, -0.22, 0.18)
    return jnp.clip(entries, -reach, reach).astype(held_as)


def setup_inputs(seed: int = 0) -> dict:
    streams_of = jax.random.split(jax.random.key(seed), 7)
    wavefield = normal_values(streams_of[0], (SHOTS, 9, NX, NY, NZ), 1.0, 6.0, ((0, 4), (2, 64)), jnp.float32)
    lame_lambda = jnp.clip(jnp.exp(math.log(2.0) - 1.3862944 * jax.random.uniform(streams_of[1], (NX, NY, NZ), jnp.float32) ** block_scale(streams_of[1], (NX, NY, NZ), ((0, 64), (1, 4)), -0.2, 0.2)), 0.5, 2.0)
    lame_mu = jnp.clip(jnp.exp(math.log(1.0) - 1.2039728 * jax.random.uniform(streams_of[2], (NX, NY, NZ), jnp.float32) ** block_scale(streams_of[2], (NX, NY, NZ), ((0, 64), (1, 4)), -0.2, 0.2)), 0.3, 1.0)
    buoyancy = jnp.clip(jnp.exp(math.log(1.0) - 0.9162907 * jax.random.uniform(streams_of[3], (NX, NY, NZ), jnp.float32) ** block_scale(streams_of[3], (NX, NY, NZ), ((0, 64), (1, 4)), -0.2, 0.2)), 0.4, 1.0)
    quality = jnp.clip(jnp.exp(math.log(2.0) - 3.6888794 * jax.random.uniform(streams_of[4], (NX, NY, NZ), jnp.float32) ** block_scale(streams_of[4], (NX, NY, NZ), ((0, 64), (1, 4)), -0.2, 0.2)), 0.05, 2.0)
    active = with_ends((jax.random.randint(streams_of[5], (STEPS, N_APER, NBY, NBZ), 0, 4) < 3).astype(jnp.int32), jax.random.fold_in(streams_of[5], 1), 0, 1)
    return dict(wavefield=wavefield, lame_lambda=lame_lambda, lame_mu=lame_mu, buoyancy=buoyancy, quality=quality, active=active)


COEF_NEAR = 1.125
COEF_FAR = -1.0 / 24.0
TIME_STEP = 0.2


def forward_rows(values, offset, length):
    return COEF_NEAR * (values[offset + 1:offset + 1 + length] - values[offset:offset + length]) + COEF_FAR * (values[offset + 2:offset + 2 + length] - values[offset - 1:offset - 1 + length])


def backward_rows(values, offset, length):
    return COEF_NEAR * (values[offset:offset + length] - values[offset - 1:offset - 1 + length]) + COEF_FAR * (values[offset + 1:offset + 1 + length] - values[offset - 2:offset - 2 + length])


def shifted(values, along, amount):
    widths = [(0, 0)] * values.ndim
    widths[along] = (2, 2)
    padded = jnp.pad(values, widths)
    return lax.slice_in_dim(padded, 2 + amount, 2 + amount + values.shape[along], axis=along)


def forward_axis(values, along):
    return COEF_NEAR * (shifted(values, along, 1) - values) + COEF_FAR * (shifted(values, along, 2) - shifted(values, along, -1))


def backward_axis(values, along):
    return COEF_NEAR * (values - shifted(values, along, -1)) + COEF_FAR * (shifted(values, along, 1) - shifted(values, along, -2))


def velocity_update(previous, stress, offset, length, buoyancy, damping, active_cells):
    def pick_rows(values):
        return values[offset:offset + length]
    grad_first = forward_rows(stress[0], offset, length) + backward_axis(pick_rows(stress[3]), 1) + backward_axis(pick_rows(stress[4]), 2)
    grad_second = backward_rows(stress[3], offset, length) + forward_axis(pick_rows(stress[1]), 1) + backward_axis(pick_rows(stress[5]), 2)
    grad_third = backward_rows(stress[4], offset, length) + backward_axis(pick_rows(stress[5]), 1) + forward_axis(pick_rows(stress[2]), 2)
    forcing = jnp.stack([grad_first, grad_second, grad_third])
    return previous + active_cells * (damping * (previous + TIME_STEP * buoyancy * forcing) - previous)


def stress_update(previous, velocity, offset, length, lambda_field, shear, damping, active_cells):
    def pick_rows(values):
        return values[offset:offset + length]
    strain_first = backward_rows(velocity[0], offset, length)
    strain_second = backward_axis(pick_rows(velocity[1]), 1)
    strain_third = backward_axis(pick_rows(velocity[2]), 2)
    dilation = strain_first + strain_second + strain_third
    shear_xy = forward_axis(pick_rows(velocity[0]), 1) + forward_rows(velocity[1], offset, length)
    shear_xz = forward_axis(pick_rows(velocity[0]), 2) + forward_rows(velocity[2], offset, length)
    shear_yz = forward_axis(pick_rows(velocity[1]), 2) + forward_axis(pick_rows(velocity[2]), 1)
    rates = jnp.stack([lambda_field * dilation + 2.0 * shear * strain_first, lambda_field * dilation + 2.0 * shear * strain_second, lambda_field * dilation + 2.0 * shear * strain_third, shear * shear_xy, shear * shear_xz, shear * shear_yz])
    return previous + active_cells * (damping * (previous + TIME_STEP * rates) - previous)


def reference(wavefield, lame_lambda, lame_mu, buoyancy, quality, active):
    damping = jnp.exp(-TIME_STEP * quality)
    length = lame_lambda.shape[0]
    rim_widths = ((0, 0), (2, 2), (0, 0), (0, 0))
    masks = []
    for moment in range(STEPS):
        blocks = active[moment].astype(jnp.float32)
        blocks = jnp.repeat(jnp.repeat(jnp.repeat(blocks, CX, axis=0), BLK, axis=1), BLK, axis=2)
        masks.append(blocks)

    def advance(values):
        for moment in range(STEPS):
            stress_pad = jnp.pad(values[3:], rim_widths)
            velocity = velocity_update(values[:3], stress_pad, 2, length, buoyancy, damping, masks[moment])
            velocity_pad = jnp.pad(velocity, rim_widths)
            stress = stress_update(values[3:], velocity_pad, 2, length, lame_lambda, lame_mu, damping, masks[moment])
            values = jnp.concatenate([velocity, stress], axis=0)
        return values

    return lax.map(advance, wavefield)
```

```python
import functools

import jax
import jax.numpy as jnp
from jax import lax
from jax.experimental import pallas as pl
from jax.experimental.pallas import tpu as pltpu
from jax.sharding import PartitionSpec as P

BLK = 32
STEPS = 4
TIME_STEP = 0.2
MESH = pl.DeviceIdType.MESH

VX, VY, VZ, SXX, SYY, SZZ, SXY, SXZ, SYZ = range(9)
LAM, MU, BUO, QUA = range(4)
ROWS = 4
NY = 128
NZ = 128
PAD = 8
LO = 2

LAYERS = {SXX: (1, 2), SXY: (2, 1), SXZ: (2, 1), VX: (2, 1), VY: (1, 2), VZ: (1, 2)}


def kernel(n_aper, n_shot, w, lam, mu, buo, qua, act, out, fields, model, masks, blocks, load_sem, act_sem, own_sem,
           gather_send, gather_recv, halo_send, halo_recv, out_sem):
    me = lax.axis_index("aper")
    shot = lax.axis_index("shot")
    has_up = me < n_aper - 1
    has_down = me > 0
    up = jnp.minimum(me + 1, n_aper - 1)
    down = jnp.maximum(me - 1, 0)
    width = NY // n_shot
    mine = pl.ds(pl.multiple_of(shot * width, width), width)
    shards = (lam, mu, buo, qua)

    def inside(f, rows):
        return fields.at[f, rows, PAD:PAD + NY, :]

    def halo(f, to_up, source=None):
        count = LAYERS[f][0 if to_up else 1]
        if to_up:
            rows, there = (LO + ROWS - count, LO - count)
        else:
            rows, there = (LO, LO + ROWS)
        if source is None:
            src = inside(f, pl.ds(rows, count))
        else:
            src = source.at[f, pl.ds(rows - LO, count)]
        side = 0 if to_up else 1
        return pltpu.make_async_remote_copy(
            src_ref=src, dst_ref=inside(f, pl.ds(there, count)), send_sem=halo_send.at[f, side],
            recv_sem=halo_recv.at[f, side], device_id=(up if to_up else down, shot), device_id_type=MESH)

    def send(f, source=None):
        @pl.when(has_up)
        def _():
            halo(f, True, source).start()

        @pl.when(has_down)
        def _():
            halo(f, False, source).start()

    def sent(f):
        @pl.when(has_up)
        def _():
            halo(f, True).wait_send()

        @pl.when(has_down)
        def _():
            halo(f, False).wait_send()

    def arrived(f):
        @pl.when(has_down)
        def _():
            halo(f, True).wait_recv()

        @pl.when(has_up)
        def _():
            halo(f, False).wait_recv()

    def share(f, step):
        peer = lax.rem(shot + step, n_shot)
        return pltpu.make_async_remote_copy(
            src_ref=shards[f], dst_ref=model.at[f, :, mine, :], send_sem=gather_send.at[f, step - 1],
            recv_sem=gather_recv.at[f, step - 1], device_id=(me, peer), device_id_type=MESH)

    loads = [pltpu.make_async_copy(w.at[f], inside(f, pl.ds(LO, ROWS)), load_sem.at[f]) for f in range(9)]
    own = [pltpu.make_async_copy(shards[f], model.at[f, :, mine, :], own_sem.at[f]) for f in range(4)]
    flags = pltpu.make_async_copy(act, blocks, act_sem)

    barrier = pltpu.get_barrier_semaphore()

    @pl.when(has_up)
    def _():
        pl.semaphore_signal(barrier, inc=1, device_id=(up, shot), device_id_type=MESH)

    @pl.when(has_down)
    def _():
        pl.semaphore_signal(barrier, inc=1, device_id=(down, shot), device_id_type=MESH)

    for step in range(1, n_shot):
        pl.semaphore_signal(barrier, inc=1, device_id=(me, lax.rem(shot + step, n_shot)), device_id_type=MESH)

    flags.start()
    for copy in loads + own:
        copy.start()

    zeros = jnp.zeros((ROWS, PAD, NZ), jnp.float32)
    for f in range(9):
        fields[f, LO:LO + ROWS, 0:PAD, :] = zeros
        fields[f, LO:LO + ROWS, PAD + NY:, :] = zeros

    @pl.when(jnp.logical_not(has_down))
    def _():
        for f in LAYERS:
            fields[f, 0:LO, PAD:PAD + NY, :] = jnp.zeros((LO, NY, NZ), jnp.float32)

    @pl.when(jnp.logical_not(has_up))
    def _():
        for f in LAYERS:
            fields[f, LO + ROWS:, PAD:PAD + NY, :] = jnp.zeros((LO, NY, NZ), jnp.float32)

    pl.semaphore_wait(barrier, n_shot - 1 + has_up.astype(jnp.int32) + has_down.astype(jnp.int32))

    for f in (SXX, SXY, SXZ):
        send(f, w)
    for f in (QUA, BUO, LAM, MU):
        for step in range(1, n_shot):
            share(f, step).start()

    lane = lax.broadcasted_iota(jnp.int32, (8, NZ), 1)
    flags.wait()
    for t in range(STEPS):
        for b in range(NY // BLK):
            on = [blocks[t, b, k, me].astype(jnp.float32) for k in range(NZ // BLK)]
            masks[t, b] = jnp.where(lane < BLK, on[0], jnp.where(lane < 2 * BLK, on[1],
                                    jnp.where(lane < 3 * BLK, on[2], on[3])))

    def gathered(f):
        own[f].wait()
        for step in range(1, n_shot):
            share(f, step).wait_recv()

    tiles = [(r, b * BLK) for b in range(NY // BLK) for r in range(ROWS)]

    gathered(QUA)
    gathered(BUO)
    for r, y in tiles:
        at = (r, slice(y, y + BLK), slice(None))
        damping = jnp.exp(-TIME_STEP * model[(QUA, *at)])
        model[(QUA, *at)] = damping - 1.0
        model[(BUO, *at)] = (TIME_STEP / 24.0) * damping * model[(BUO, *at)]

    wide = lax.broadcasted_iota(jnp.int32, (BLK, NZ), 1)

    def at(f, r, y, dy=0):
        return fields[f, LO + r, PAD + y + dy:PAD + y + dy + BLK, :]

    def near_far(back, back2, here, ahead, ahead2, forward):
        if forward:
            return ahead - here, ahead2 - back
        return here - back, ahead - back2

    def along_x(f, r, y, forward):
        if forward:
            return at(f, r + 1, y) - at(f, r, y), at(f, r + 2, y) - at(f, r - 1, y)
        return at(f, r, y) - at(f, r - 1, y), at(f, r + 1, y) - at(f, r - 2, y)

    def along_y(f, r, y, forward):
        if forward:
            return at(f, r, y, 1) - at(f, r, y), at(f, r, y, 2) - at(f, r, y, -1)
        return at(f, r, y) - at(f, r, y, -1), at(f, r, y, 1) - at(f, r, y, -2)

    def along_z(f, r, y, forward):
        here = at(f, r, y)

        def moved(k):
            turned = pltpu.roll(here, (-k) % NZ, 1)
            return jnp.where(wide < NZ - k if k > 0 else wide >= -k, turned, 0.0)

        if forward:
            return moved(1) - here, moved(2) - moved(-1)
        return here - moved(-1), moved(1) - moved(-2)

    def total(*parts):
        near = sum(p[0] for p in parts[1:]) + parts[0][0]
        far = sum(p[1] for p in parts[1:]) + parts[0][1]
        return 27.0 * near - far

    def mask_of(t, y):
        return jnp.tile(masks[t, y // BLK], (BLK // 8, 1))

    def keep(t, r, y, mask):
        return 1.0 + mask * model[QUA, r, y:y + BLK, :]

    def put(f, r, y, value):
        fields[f, LO + r, PAD + y:PAD + y + BLK, :] = value

    def velocity(t, f, gradient):
        for r, y in tiles:
            mask = mask_of(t, y)
            factor = mask * model[BUO, r, y:y + BLK, :]
            put(f, r, y, keep(t, r, y, mask) * at(f, r, y) + factor * gradient(r, y))

    def normal(t):
        for r, y in tiles:
            mask = mask_of(t, y)
            kept = keep(t, r, y, mask)
            shear = mask * model[MU, r, y:y + BLK, :]
            twice = shear + shear
            strain = [total(along_x(VX, r, y, False)), total(along_y(VY, r, y, False)), total(along_z(VZ, r, y, False))]
            swell = mask * model[LAM, r, y:y + BLK, :] * (strain[0] + strain[1] + strain[2])
            for f, part in zip((SXX, SYY, SZZ), strain):
                put(f, r, y, kept * at(f, r, y) + (swell + twice * part))

    def sheared(t, f, gradient):
        for r, y in tiles:
            mask = mask_of(t, y)
            factor = mask * model[MU, r, y:y + BLK, :]
            put(f, r, y, keep(t, r, y, mask) * at(f, r, y) + factor * gradient(r, y))

    for copy in loads:
        copy.wait()

    def body(t, carry):
        again = t < STEPS - 1

        def reuse(f):
            @pl.when(t > 0)
            def _():
                sent(f)

        arrived(SXX)
        reuse(VX)
        velocity(t, VX, lambda r, y: total(along_x(SXX, r, y, True), along_y(SXY, r, y, False), along_z(SXZ, r, y, False)))
        send(VX)
        arrived(SXY)
        reuse(VY)
        velocity(t, VY, lambda r, y: total(along_x(SXY, r, y, False), along_y(SYY, r, y, True), along_z(SYZ, r, y, False)))
        send(VY)
        arrived(SXZ)
        reuse(VZ)
        velocity(t, VZ, lambda r, y: total(along_x(SXZ, r, y, False), along_y(SYZ, r, y, False), along_z(SZZ, r, y, True)))
        send(VZ)

        @pl.when(t == 0)
        def _():
            gathered(LAM)
            gathered(MU)
            for r, y in tiles:
                spot = (r, slice(y, y + BLK), slice(None))
                factor = (TIME_STEP / 24.0) * (model[(QUA, *spot)] + 1.0)
                model[(LAM, *spot)] = factor * model[(LAM, *spot)]
                model[(MU, *spot)] = factor * model[(MU, *spot)]

        sheared(t, SYZ, lambda r, y: total(along_z(VY, r, y, True), along_y(VZ, r, y, True)))
        arrived(VX)
        sent(SXX)
        normal(t)

        @pl.when(again)
        def _():
            send(SXX)

        arrived(VY)
        sent(SXY)
        sheared(t, SXY, lambda r, y: total(along_y(VX, r, y, True), along_x(VY, r, y, True)))

        @pl.when(again)
        def _():
            send(SXY)

        arrived(VZ)
        sent(SXZ)
        sheared(t, SXZ, lambda r, y: total(along_z(VX, r, y, True), along_x(VZ, r, y, True)))

        @pl.when(again)
        def _():
            send(SXZ)

        return carry

    lax.fori_loop(0, STEPS, body, 0)

    stores = [pltpu.make_async_copy(inside(f, pl.ds(LO, ROWS)), out.at[f], out_sem.at[f]) for f in range(9)]
    for copy in stores:
        copy.start()
    for f in (VX, VY, VZ):
        sent(f)
    for f in range(4):
        for step in range(1, n_shot):
            share(f, step).wait_send()
    for copy in stores:
        copy.wait()


def solution(mesh):
    n_aper, n_shot = mesh.shape["aper"], mesh.shape["shot"]

    def per_device(wavefield, lame_lambda, lame_mu, buoyancy, quality, active):
        hbm = pl.BlockSpec(memory_space=pltpu.HBM)
        result = pl.pallas_call(
            functools.partial(kernel, n_aper, n_shot),
            out_shape=jax.ShapeDtypeStruct((9, ROWS, NY, NZ), jnp.float32),
            in_specs=[hbm] * 6,
            out_specs=pl.BlockSpec(memory_space=pl.ANY),
            scratch_shapes=[
                pltpu.VMEM((9, ROWS + 2 * LO, NY + 2 * PAD, NZ), jnp.float32),
                pltpu.VMEM((4, ROWS, NY, NZ), jnp.float32),
                pltpu.VMEM((STEPS, NY // BLK, 8, NZ), jnp.float32),
                pltpu.SMEM((STEPS, NY // BLK, NZ // BLK, n_aper), jnp.int32),
                pltpu.SemaphoreType.DMA((9,)),
                pltpu.SemaphoreType.DMA,
                pltpu.SemaphoreType.DMA((4,)),
                pltpu.SemaphoreType.DMA((4, n_shot - 1)),
                pltpu.SemaphoreType.DMA((4, n_shot - 1)),
                pltpu.SemaphoreType.DMA((9, 2)),
                pltpu.SemaphoreType.DMA((9, 2)),
                pltpu.SemaphoreType.DMA((9,)),
            ],
            compiler_params=pltpu.CompilerParams(
                collective_id=0, has_side_effects=True, vmem_limit_bytes=60 * 1024 * 1024
            ),
            name="elastic_steps",
        )(wavefield[0], lame_lambda, lame_mu, buoyancy, quality, jnp.transpose(active, (0, 2, 3, 1)))
        return result[None]

    return jax.shard_map(
        per_device,
        mesh=mesh,
        in_specs=(
            P("shot", None, "aper", None, None),
            P("aper", "shot", None),
            P("aper", "shot", None),
            P("aper", "shot", None),
            P("aper", "shot", None),
            P(),
        ),
        out_specs=P("shot", None, "aper", None, None),
        check_vma=False,
    )
```

```python
import functools

import jax
import jax.numpy as jnp
from jax import lax
from jax.experimental import pallas as pl
from jax.experimental.pallas import tpu as pltpu
from jax.sharding import PartitionSpec as P

BLK = 32
STEPS = 4
TIME_STEP = 0.2
MESH = pl.DeviceIdType.MESH

VX, VY, VZ, SXX, SYY, SZZ, SXY, SXZ, SYZ = range(9)
LAM, MU, BUO, QUA = range(4)
ROWS = 4
NY = 128
NZ = 128
PAD = 8
LO = 2

PLANE = 16
SIDE = 4
PIECES = (64, 32, 32)

FORWARD = ((SXX, SXY), (SXZ,), (), (VX, VY), (VZ,), ())

LAYERS = {SXX: (1, 2), SXY: (2, 1), SXZ: (2, 1), VX: (2, 1), VY: (1, 2), VZ: (1, 2)}


def kernel(n_aper, n_shot, w, lam, mu, buo, qua, act, out, fields, model, masks, blocks, load_sem, act_sem, own_sem,
           gather_send, gather_recv, halo_send, halo_recv, out_sem, relay, leg_send, leg_recv, onward_send):
    me = lax.axis_index("aper")
    shot = lax.axis_index("shot")
    has_up = me < n_aper - 1
    has_down = me > 0
    up = jnp.minimum(me + 1, n_aper - 1)
    down = jnp.maximum(me - 1, 0)
    width = NY // n_shot
    shards = (lam, mu, buo, qua)

    def inside(f, rows):
        return fields.at[f, rows, PAD:PAD + NY, :]

    local = lax.rem(me, PLANE)
    last_plane = me >= n_aper - PLANE
    first_plane = me < PLANE
    crosses_up = jnp.logical_and(local == PLANE - 1, jnp.logical_not(last_plane))
    crosses_down = jnp.logical_and(local == 0, jnp.logical_not(first_plane))
    plain_up = jnp.logical_and(has_up, jnp.logical_not(crosses_up))
    plain_down = jnp.logical_and(has_down, jnp.logical_not(crosses_down))
    not_last, not_first = jnp.logical_not(last_plane), jnp.logical_not(first_plane)
    roles = [
        (jnp.logical_and(local == PLANE - SIDE, not_last), SIDE - 1, SIDE, True, 1),
        (jnp.logical_and(local == SIDE - 1, not_last), PLANE - SIDE, PLANE - SIDE + 1, True, 2),
        (jnp.logical_and(local == SIDE - 1, not_first), 1 - SIDE, -SIDE, False, 1),
        (jnp.logical_and(local == PLANE - SIDE, not_first), SIDE - PLANE, SIDE - PLANE - 1, False, 2),
    ]
    starts = [sum(PIECES[:k]) for k in range(len(PIECES))]

    def clipped(index):
        return jnp.clip(index, 0, n_aper - 1)

    def span(k):
        return pl.ds(PAD + starts[k], PIECES[k])

    def edge(f, to_up):
        count = LAYERS[f][0 if to_up else 1]
        if to_up:
            return pl.ds(LO + ROWS - count, count), pl.ds(LO - count, count)
        return pl.ds(LO, count), pl.ds(LO + ROWS, count)

    def leaving(f, to_up, ys, source):
        rows = edge(f, to_up)[0]
        if source is None:
            return fields.at[f, rows, ys, :]
        return source.at[f, pl.ds(rows.start - LO, rows.size), pl.ds(ys.start - PAD, ys.size), :]

    def halo(f, to_up, k=None, source=None):
        ys = pl.ds(PAD, NY) if k is None else span(k)
        side = 0 if to_up else 1
        return pltpu.make_async_remote_copy(
            src_ref=leaving(f, to_up, ys, source), dst_ref=fields.at[f, edge(f, to_up)[1], ys, :],
            send_sem=halo_send.at[f, side], recv_sem=halo_recv.at[f, side, k or 0],
            device_id=(up if to_up else down, shot), device_id_type=MESH)

    def leg(f, to_up, k, source=None, t=0):
        away = SIDE - 1 if k == 1 else PLANE - SIDE
        target = me - away if to_up else me + away
        return pltpu.make_async_remote_copy(
            src_ref=leaving(f, to_up, span(k), source),
            dst_ref=relay.at[t, 0 if to_up else 1, f, pl.ds(0, edge(f, to_up)[0].size), pl.ds(0, PIECES[k]), :],
            send_sem=leg_send.at[f, k - 1], recv_sem=leg_recv.at[f, 0 if to_up else 1], device_id=(clipped(target), shot), device_id_type=MESH)

    def onward(f, role, t=0):
        _, _, offset, to_up, k = role
        rows, side = edge(f, to_up)[1], 0 if to_up else 1
        return pltpu.make_async_remote_copy(
            src_ref=relay.at[t, side, f, pl.ds(0, rows.size), pl.ds(0, PIECES[k]), :], dst_ref=fields.at[f, rows, span(k), :],
            send_sem=onward_send.at[f, side], recv_sem=halo_recv.at[f, side, k],
            device_id=(clipped(me + offset), shot), device_id_type=MESH)

    def send(f, t, source=None):
        for to_up, crosses, plain in ((True, crosses_up, plain_up), (False, crosses_down, plain_down)):
            @pl.when(crosses)
            def _():
                leg(f, to_up, 1, source, t).start()
                leg(f, to_up, 2, source, t).start()
                halo(f, to_up, 0, source).start()

            @pl.when(plain)
            def _():
                halo(f, to_up, None, source).start()

    def sent(f):
        for to_up, crosses, plain in ((True, crosses_up, plain_up), (False, crosses_down, plain_down)):
            @pl.when(crosses)
            def _():
                leg(f, to_up, 1).wait_send()
                leg(f, to_up, 2).wait_send()
                halo(f, to_up, 0).wait_send()

            @pl.when(plain)
            def _():
                halo(f, to_up).wait_send()

    def arrived(f):
        for to_up, crosses, plain in ((True, crosses_down, plain_down), (False, crosses_up, plain_up)):
            @pl.when(crosses)
            def _():
                for k in range(len(PIECES)):
                    halo(f, to_up, k).wait_recv()

            @pl.when(plain)
            def _():
                halo(f, to_up).wait_recv()

    def forward(t, *some):
        for f in some:
            for role in roles:
                @pl.when(role[0])
                def _():
                    @pl.when(t > 0)
                    def _():
                        onward(f, role).wait_send()

                    leg(f, role[3], role[4]).wait_recv()
                    onward(f, role, t).start()

    partner = shot + 1 - 2 * lax.rem(shot, 2)
    across = lax.rem(shot + 2, n_shot)

    def shard_rows(owner):
        return pl.ds(pl.multiple_of(owner * width, width), width)

    def share(f, hop):
        place = model.at[f, :, shard_rows(across if hop == 2 else shot), :]
        return pltpu.make_async_remote_copy(
            src_ref=place if hop == 2 else shards[f], dst_ref=place, send_sem=gather_send.at[f, hop],
            recv_sem=gather_recv.at[f, hop], device_id=(me, across if hop == 1 else partner), device_id_type=MESH)

    def pass_on(f):
        share(f, 1).wait_recv()
        share(f, 2).start()

    loads = [pltpu.make_async_copy(w.at[f], inside(f, pl.ds(LO, ROWS)), load_sem.at[f]) for f in range(9)]
    own = [pltpu.make_async_copy(shards[f], model.at[f, :, shard_rows(shot), :], own_sem.at[f]) for f in range(4)]
    flags = pltpu.make_async_copy(act, blocks, act_sem)

    barrier = pltpu.get_barrier_semaphore()

    greeted = [(has_up, me + 1), (has_down, me - 1)]
    for crossing, sign in ((crosses_up, 1), (crosses_down, -1)):
        greeted += [(crossing, me - sign * (SIDE - 1)), (crossing, me - sign * (PLANE - SIDE)),
                    (crossing, me + sign * SIDE), (crossing, me + sign * (PLANE - SIDE + 1))]
    for here, origin, target, _, _ in roles:
        greeted += [(here, me + origin), (here, me + target)]
    for here, whom in greeted:
        @pl.when(here)
        def _():
            pl.semaphore_signal(barrier, inc=1, device_id=(clipped(whom), shot), device_id_type=MESH)

    for peer in (partner, across):
        pl.semaphore_signal(barrier, inc=1, device_id=(me, peer), device_id_type=MESH)

    flags.start()
    for copy in loads + own:
        copy.start()

    zeros = jnp.zeros((ROWS, PAD, NZ), jnp.float32)
    for f in range(9):
        fields[f, LO:LO + ROWS, 0:PAD, :] = zeros
        fields[f, LO:LO + ROWS, PAD + NY:, :] = zeros

    @pl.when(jnp.logical_not(has_down))
    def _():
        for f in LAYERS:
            fields[f, 0:LO, PAD:PAD + NY, :] = jnp.zeros((LO, NY, NZ), jnp.float32)

    @pl.when(jnp.logical_not(has_up))
    def _():
        for f in LAYERS:
            fields[f, LO + ROWS:, PAD:PAD + NY, :] = jnp.zeros((LO, NY, NZ), jnp.float32)

    pl.semaphore_wait(barrier, 2 + sum(here.astype(jnp.int32) for here, _ in greeted))

    for f in (QUA, BUO):
        for hop in (1, 0):
            share(f, hop).start()
    for f in (SXX, SXY, SXZ):
        send(f, 0, w)
    for f in (LAM, MU):
        for hop in (1, 0):
            share(f, hop).start()

    lane = lax.broadcasted_iota(jnp.int32, (8, NZ), 1)
    flags.wait()
    for t in range(STEPS):
        for b in range(NY // BLK):
            on = [blocks[t, b, k, me].astype(jnp.float32) for k in range(NZ // BLK)]
            masks[t, b] = jnp.where(lane < BLK, on[0], jnp.where(lane < 2 * BLK, on[1],
                                    jnp.where(lane < 3 * BLK, on[2], on[3])))

    def gathered(f):
        own[f].wait()
        for hop in (0, 2):
            share(f, hop).wait_recv()
        share(f, 2).wait_send()

    tiles = [(r, b * BLK) for b in range(NY // BLK) for r in range(ROWS)]

    pass_on(QUA)
    pass_on(BUO)
    gathered(QUA)
    gathered(BUO)
    for r, y in tiles:
        at = (r, slice(y, y + BLK), slice(None))
        damping = jnp.exp(-TIME_STEP * model[(QUA, *at)])
        model[(QUA, *at)] = damping - 1.0
        model[(BUO, *at)] = (TIME_STEP / 24.0) * damping * model[(BUO, *at)]

    wide = lax.broadcasted_iota(jnp.int32, (BLK, NZ), 1)

    def at(f, r, y, dy=0):
        return fields[f, LO + r, PAD + y + dy:PAD + y + dy + BLK, :]

    def along_x(f, r, y, forward):
        if forward:
            return at(f, r + 1, y) - at(f, r, y), at(f, r + 2, y) - at(f, r - 1, y)
        return at(f, r, y) - at(f, r - 1, y), at(f, r + 1, y) - at(f, r - 2, y)

    def along_y(f, r, y, forward):
        if forward:
            return at(f, r, y, 1) - at(f, r, y), at(f, r, y, 2) - at(f, r, y, -1)
        return at(f, r, y) - at(f, r, y, -1), at(f, r, y, 1) - at(f, r, y, -2)

    def along_z(f, r, y, forward):
        here = at(f, r, y)

        def moved(k):
            turned = pltpu.roll(here, (-k) % NZ, 1)
            return jnp.where(wide < NZ - k if k > 0 else wide >= -k, turned, 0.0)

        if forward:
            return moved(1) - here, moved(2) - moved(-1)
        return here - moved(-1), moved(1) - moved(-2)

    def total(*parts):
        near, far = parts[0]
        for more in parts[1:]:
            near, far = near + more[0], far + more[1]
        return 27.0 * near - far

    def mask_of(t, y):
        return jnp.tile(masks[t, y // BLK], (BLK // 8, 1))

    def keep(t, r, y, mask):
        return 1.0 + mask * model[QUA, r, y:y + BLK, :]

    def put(f, r, y, value):
        fields[f, LO + r, PAD + y:PAD + y + BLK, :] = value

    def begin(t, f, coefficient, gradient):
        for r, y in tiles:
            mask = mask_of(t, y)
            factor = mask * model[coefficient, r, y:y + BLK, :]
            put(f, r, y, keep(t, r, y, mask) * at(f, r, y) + factor * gradient(r, y))

    def finish(t, f, coefficient, gradient):
        for r, y in tiles:
            factor = mask_of(t, y) * model[coefficient, r, y:y + BLK, :]
            put(f, r, y, at(f, r, y) + factor * gradient(r, y))

    def begin_normal(t):
        for r, y in tiles:
            mask = mask_of(t, y)
            kept = keep(t, r, y, mask)
            shear = mask * model[MU, r, y:y + BLK, :]
            twice = shear + shear
            second, third = total(along_y(VY, r, y, False)), total(along_z(VZ, r, y, False))
            swell = mask * model[LAM, r, y:y + BLK, :] * (second + third)
            put(SXX, r, y, kept * at(SXX, r, y) + swell)
            put(SYY, r, y, kept * at(SYY, r, y) + (swell + twice * second))
            put(SZZ, r, y, kept * at(SZZ, r, y) + (swell + twice * third))

    def finish_normal(t):
        for r, y in tiles:
            mask = mask_of(t, y)
            first = mask * total(along_x(VX, r, y, False))
            shear = model[MU, r, y:y + BLK, :]
            swell = model[LAM, r, y:y + BLK, :] * first
            put(SXX, r, y, at(SXX, r, y) + (swell + (shear + shear) * first))
            put(SYY, r, y, at(SYY, r, y) + swell)
            put(SZZ, r, y, at(SZZ, r, y) + swell)

    for copy in loads:
        copy.wait()

    def body(t, carry):
        again = t < STEPS - 1

        def reuse(f):
            @pl.when(t > 0)
            def _():
                sent(f)

        reuse(VX)
        begin(t, VX, BUO, lambda r, y: total(along_y(SXY, r, y, False), along_z(SXZ, r, y, False)))
        reuse(VY)
        begin(t, VY, BUO, lambda r, y: total(along_y(SYY, r, y, True), along_z(SYZ, r, y, False)))
        reuse(VZ)
        begin(t, VZ, BUO, lambda r, y: total(along_y(SYZ, r, y, False), along_z(SZZ, r, y, True)))
        forward(t, *FORWARD[0])
        arrived(SXX)
        finish(t, VX, BUO, lambda r, y: total(along_x(SXX, r, y, True)))
        send(VX, t)
        forward(t, *FORWARD[1])
        arrived(SXY)
        finish(t, VY, BUO, lambda r, y: total(along_x(SXY, r, y, False)))
        send(VY, t)

        @pl.when(t == 0)
        def _():
            pass_on(LAM)
            pass_on(MU)

        forward(t, *FORWARD[2])
        arrived(SXZ)
        finish(t, VZ, BUO, lambda r, y: total(along_x(SXZ, r, y, False)))
        send(VZ, t)

        @pl.when(t == 0)
        def _():
            gathered(LAM)
            gathered(MU)
            for r, y in tiles:
                spot = (r, slice(y, y + BLK), slice(None))
                factor = (TIME_STEP / 24.0) * (model[(QUA, *spot)] + 1.0)
                model[(LAM, *spot)] = factor * model[(LAM, *spot)]
                model[(MU, *spot)] = factor * model[(MU, *spot)]

        sent(SXX)
        begin_normal(t)
        sent(SXY)
        begin(t, SXY, MU, lambda r, y: total(along_y(VX, r, y, True)))
        sent(SXZ)
        begin(t, SXZ, MU, lambda r, y: total(along_z(VX, r, y, True)))
        begin(t, SYZ, MU, lambda r, y: total(along_z(VY, r, y, True), along_y(VZ, r, y, True)))
        forward(t, *FORWARD[3])
        arrived(VX)
        finish_normal(t)

        @pl.when(again)
        def _():
            send(SXX, t + 1)

        forward(t, *FORWARD[4])
        arrived(VY)
        finish(t, SXY, MU, lambda r, y: total(along_x(VY, r, y, True)))

        @pl.when(again)
        def _():
            send(SXY, t + 1)

        forward(t, *FORWARD[5])
        arrived(VZ)
        finish(t, SXZ, MU, lambda r, y: total(along_x(VZ, r, y, True)))

        @pl.when(again)
        def _():
            send(SXZ, t + 1)

        return carry

    lax.fori_loop(0, STEPS, body, 0)

    stores = [pltpu.make_async_copy(inside(f, pl.ds(LO, ROWS)), out.at[f], out_sem.at[f]) for f in range(9)]
    for copy in stores:
        copy.start()
    for f in (VX, VY, VZ):
        sent(f)
    for role in roles:
        @pl.when(role[0])
        def _():
            for f in LAYERS:
                onward(f, role).wait_send()

    for f in range(4):
        for hop in range(2):
            share(f, hop).wait_send()
    for copy in stores:
        copy.wait()


def solution(mesh):
    n_aper, n_shot = mesh.shape["aper"], mesh.shape["shot"]

    def per_device(wavefield, lame_lambda, lame_mu, buoyancy, quality, active):
        hbm = pl.BlockSpec(memory_space=pltpu.HBM)
        result = pl.pallas_call(
            functools.partial(kernel, n_aper, n_shot),
            out_shape=jax.ShapeDtypeStruct((9, ROWS, NY, NZ), jnp.float32),
            in_specs=[hbm] * 6,
            out_specs=pl.BlockSpec(memory_space=pl.ANY),
            scratch_shapes=[
                pltpu.VMEM((9, ROWS + 2 * LO, NY + 2 * PAD, NZ), jnp.float32),
                pltpu.VMEM((4, ROWS, NY, NZ), jnp.float32),
                pltpu.VMEM((STEPS, NY // BLK, 8, NZ), jnp.float32),
                pltpu.SMEM((STEPS, NY // BLK, NZ // BLK, n_aper), jnp.int32),
                pltpu.SemaphoreType.DMA((9,)),
                pltpu.SemaphoreType.DMA,
                pltpu.SemaphoreType.DMA((4,)),
                pltpu.SemaphoreType.DMA((4, 3)),
                pltpu.SemaphoreType.DMA((4, 3)),
                pltpu.SemaphoreType.DMA((9, 2)),
                pltpu.SemaphoreType.DMA((9, 2, 3)),
                pltpu.SemaphoreType.DMA((9,)),
                pltpu.VMEM((STEPS, 2, 9, LO, max(PIECES[1:]), NZ), jnp.float32),
                pltpu.SemaphoreType.DMA((9, 2)),
                pltpu.SemaphoreType.DMA((9, 2)),
                pltpu.SemaphoreType.DMA((9, 2)),
            ],
            compiler_params=pltpu.CompilerParams(
                collective_id=0, has_side_effects=True, vmem_limit_bytes=60 * 1024 * 1024
            ),
            name="elastic_steps",
        )(wavefield[0], lame_lambda, lame_mu, buoyancy, quality, jnp.transpose(active, (0, 2, 3, 1)))
        return result[None]

    return jax.shard_map(
        per_device,
        mesh=mesh,
        in_specs=(
            P("shot", None, "aper", None, None),
            P("aper", "shot", None),
            P("aper", "shot", None),
            P("aper", "shot", None),
            P("aper", "shot", None),
            P(),
        ),
        out_specs=P("shot", None, "aper", None, None),
        check_vma=False,
    )
```

```python
import functools

import jax
import jax.numpy as jnp
from jax import lax
from jax.experimental import pallas as pl
from jax.experimental.pallas import tpu as pltpu
from jax.sharding import PartitionSpec as P

BLK = 32
STEPS = 4
TIME_STEP = 0.2
MESH = pl.DeviceIdType.MESH

VX, VY, VZ, SXX, SYY, SZZ, SXY, SXZ, SYZ = range(9)
LAM, MU, BUO, QUA = range(4)
ROWS = 4
NY = 128
NZ = 128
PAD = 8
LO = 2

PLANE = 16
SIDE = 4
PIECES = (56, 32, 40)

FIRST = 0
FORWARD = ((SXX, SXY), (SXZ,), (), (VX, VY), (VZ,), ())

LAYERS = {SXX: (1, 2), SXY: (2, 1), SXZ: (2, 1), VX: (2, 1), VY: (1, 2), VZ: (1, 2)}


def kernel(n_aper, n_shot, w, lam, mu, buo, qua, act, out, fields, model, masks, blocks, load_sem, act_sem, own_sem,
           gather_send, gather_recv, halo_send, halo_recv, out_sem, relay, leg_send, leg_recv, onward_send):
    me = lax.axis_index("aper")
    shot = lax.axis_index("shot")
    has_up = me < n_aper - 1
    has_down = me > 0
    up = jnp.minimum(me + 1, n_aper - 1)
    down = jnp.maximum(me - 1, 0)
    width = NY // n_shot
    shards = (lam, mu, buo, qua)

    def inside(f, rows):
        return fields.at[f, rows, PAD:PAD + NY, :]

    local = lax.rem(me, PLANE)
    last_plane = me >= n_aper - PLANE
    first_plane = me < PLANE
    crosses_up = jnp.logical_and(local == PLANE - 1, jnp.logical_not(last_plane))
    crosses_down = jnp.logical_and(local == 0, jnp.logical_not(first_plane))
    plain_up = jnp.logical_and(has_up, jnp.logical_not(crosses_up))
    plain_down = jnp.logical_and(has_down, jnp.logical_not(crosses_down))
    not_last, not_first = jnp.logical_not(last_plane), jnp.logical_not(first_plane)
    roles = [
        (jnp.logical_and(local == PLANE - SIDE, not_last), SIDE - 1, SIDE, True, 1),
        (jnp.logical_and(local == SIDE - 1, not_last), PLANE - SIDE, PLANE - SIDE + 1, True, 2),
        (jnp.logical_and(local == SIDE - 1, not_first), 1 - SIDE, -SIDE, False, 1),
        (jnp.logical_and(local == PLANE - SIDE, not_first), SIDE - PLANE, SIDE - PLANE - 1, False, 2),
    ]
    starts = [sum(PIECES[:k]) for k in range(len(PIECES))]

    def clipped(index):
        return jnp.clip(index, 0, n_aper - 1)

    def span(k):
        return pl.ds(PAD + starts[k], PIECES[k])

    def edge(f, to_up):
        count = LAYERS[f][0 if to_up else 1]
        if to_up:
            return pl.ds(LO + ROWS - count, count), pl.ds(LO - count, count)
        return pl.ds(LO, count), pl.ds(LO + ROWS, count)

    def leaving(f, to_up, ys, source):
        rows = edge(f, to_up)[0]
        if source is None:
            return fields.at[f, rows, ys, :]
        return source.at[f, pl.ds(rows.start - LO, rows.size), pl.ds(ys.start - PAD, ys.size), :]

    def halo(f, to_up, k=None, source=None):
        ys = pl.ds(PAD, NY) if k is None else span(k)
        side = 0 if to_up else 1
        return pltpu.make_async_remote_copy(
            src_ref=leaving(f, to_up, ys, source), dst_ref=fields.at[f, edge(f, to_up)[1], ys, :],
            send_sem=halo_send.at[f, side], recv_sem=halo_recv.at[f, side, k or 0],
            device_id=(up if to_up else down, shot), device_id_type=MESH)

    def leg(f, to_up, k, source=None, t=0):
        away = SIDE - 1 if k == 1 else PLANE - SIDE
        target = me - away if to_up else me + away
        return pltpu.make_async_remote_copy(
            src_ref=leaving(f, to_up, span(k), source),
            dst_ref=relay.at[t, 0 if to_up else 1, f, pl.ds(0, edge(f, to_up)[0].size), pl.ds(0, PIECES[k]), :],
            send_sem=leg_send.at[f, k - 1], recv_sem=leg_recv.at[f, 0 if to_up else 1], device_id=(clipped(target), shot), device_id_type=MESH)

    def onward(f, role, t=0):
        _, _, offset, to_up, k = role
        rows, side = edge(f, to_up)[1], 0 if to_up else 1
        return pltpu.make_async_remote_copy(
            src_ref=relay.at[t, side, f, pl.ds(0, rows.size), pl.ds(0, PIECES[k]), :], dst_ref=fields.at[f, rows, span(k), :],
            send_sem=onward_send.at[f, side], recv_sem=halo_recv.at[f, side, k],
            device_id=(clipped(me + offset), shot), device_id_type=MESH)

    def send(f, t, source=None):
        for to_up, crosses, plain in ((True, crosses_up, plain_up), (False, crosses_down, plain_down)):
            @pl.when(crosses)
            def _():
                leg(f, to_up, 1, source, t).start()
                leg(f, to_up, 2, source, t).start()
                halo(f, to_up, 0, source).start()

            @pl.when(plain)
            def _():
                halo(f, to_up, None, source).start()

    def sent(f):
        for to_up, crosses, plain in ((True, crosses_up, plain_up), (False, crosses_down, plain_down)):
            @pl.when(crosses)
            def _():
                leg(f, to_up, 1).wait_send()
                leg(f, to_up, 2).wait_send()
                halo(f, to_up, 0).wait_send()

            @pl.when(plain)
            def _():
                halo(f, to_up).wait_send()

    def arrived(f):
        for to_up, crosses, plain in ((True, crosses_down, plain_down), (False, crosses_up, plain_up)):
            @pl.when(crosses)
            def _():
                for k in range(len(PIECES)):
                    halo(f, to_up, k).wait_recv()

            @pl.when(plain)
            def _():
                halo(f, to_up).wait_recv()

    def relayed(t, *some):
        for f in some:
            for role in roles:
                @pl.when(role[0])
                def _():
                    if t is not FIRST:
                        @pl.when(t > 0)
                        def _():
                            onward(f, role).wait_send()

                    leg(f, role[3], role[4]).wait_recv()
                    onward(f, role, t).start()

    def forward(t, *some):
        now = [f for f in some if f in (VX, VY, VZ)]
        if now:
            relayed(t, *now)
        later = [f for f in some if f not in now]
        if later:
            @pl.when(t > 0)
            def _():
                relayed(t, *later)

    partner = shot + 1 - 2 * lax.rem(shot, 2)
    across = lax.rem(shot + 2, n_shot)

    def shard_rows(owner):
        return pl.ds(pl.multiple_of(owner * width, width), width)

    def share(f, hop):
        place = model.at[f, :, shard_rows(across if hop == 2 else shot), :]
        return pltpu.make_async_remote_copy(
            src_ref=place if hop == 2 else shards[f], dst_ref=place, send_sem=gather_send.at[f, hop],
            recv_sem=gather_recv.at[f, hop], device_id=(me, across if hop == 1 else partner), device_id_type=MESH)

    def pass_on(f):
        share(f, 1).wait_recv()
        share(f, 2).start()

    loads = [pltpu.make_async_copy(w.at[f], inside(f, pl.ds(LO, ROWS)), load_sem.at[f]) for f in range(9)]
    own = [pltpu.make_async_copy(shards[f], model.at[f, :, shard_rows(shot), :], own_sem.at[f]) for f in range(4)]
    flags = pltpu.make_async_copy(act, blocks, act_sem)

    barrier = pltpu.get_barrier_semaphore()

    greeted = [(has_up, me + 1), (has_down, me - 1)]
    for crossing, sign in ((crosses_up, 1), (crosses_down, -1)):
        greeted += [(crossing, me - sign * (SIDE - 1)), (crossing, me - sign * (PLANE - SIDE)),
                    (crossing, me + sign * SIDE), (crossing, me + sign * (PLANE - SIDE + 1))]
    for here, origin, target, _, _ in roles:
        greeted += [(here, me + origin), (here, me + target)]
    for here, whom in greeted:
        @pl.when(here)
        def _():
            pl.semaphore_signal(barrier, inc=1, device_id=(clipped(whom), shot), device_id_type=MESH)

    for peer in (partner, across):
        pl.semaphore_signal(barrier, inc=1, device_id=(me, peer), device_id_type=MESH)

    flags.start()
    for copy in loads + own:
        copy.start()

    zeros = jnp.zeros((ROWS, PAD, NZ), jnp.float32)
    for f in range(9):
        fields[f, LO:LO + ROWS, 0:PAD, :] = zeros
        fields[f, LO:LO + ROWS, PAD + NY:, :] = zeros

    @pl.when(jnp.logical_not(has_down))
    def _():
        for f in LAYERS:
            fields[f, 0:LO, PAD:PAD + NY, :] = jnp.zeros((LO, NY, NZ), jnp.float32)

    @pl.when(jnp.logical_not(has_up))
    def _():
        for f in LAYERS:
            fields[f, LO + ROWS:, PAD:PAD + NY, :] = jnp.zeros((LO, NY, NZ), jnp.float32)

    pl.semaphore_wait(barrier, 2 + sum(here.astype(jnp.int32) for here, _ in greeted))

    for f in (QUA, BUO):
        for hop in (1, 0):
            share(f, hop).start()
    for f in (SXX, SXY, SXZ):
        send(f, 0, w)
    for f in (LAM, MU):
        for hop in (1, 0):
            share(f, hop).start()

    lane = lax.broadcasted_iota(jnp.int32, (8, NZ), 1)
    flags.wait()
    for t in range(STEPS):
        for b in range(NY // BLK):
            on = [blocks[t, b, k, me].astype(jnp.float32) for k in range(NZ // BLK)]
            masks[t, b] = jnp.where(lane < BLK, on[0], jnp.where(lane < 2 * BLK, on[1],
                                    jnp.where(lane < 3 * BLK, on[2], on[3])))

    relayed(FIRST, SXX, SXY, SXZ)

    def gathered(f):
        own[f].wait()
        for hop in (0, 2):
            share(f, hop).wait_recv()
        share(f, 2).wait_send()

    tiles = [(r, b * BLK) for b in range(NY // BLK) for r in range(ROWS)]

    pass_on(QUA)
    pass_on(BUO)
    gathered(QUA)
    gathered(BUO)
    for r, y in tiles:
        at = (r, slice(y, y + BLK), slice(None))
        damping = jnp.exp(-TIME_STEP * model[(QUA, *at)])
        model[(QUA, *at)] = damping - 1.0
        model[(BUO, *at)] = (TIME_STEP / 24.0) * damping * model[(BUO, *at)]

    wide = lax.broadcasted_iota(jnp.int32, (BLK, NZ), 1)

    def at(f, r, y, dy=0):
        return fields[f, LO + r, PAD + y + dy:PAD + y + dy + BLK, :]

    def along_x(f, r, y, forward):
        if forward:
            return at(f, r + 1, y) - at(f, r, y), at(f, r + 2, y) - at(f, r - 1, y)
        return at(f, r, y) - at(f, r - 1, y), at(f, r + 1, y) - at(f, r - 2, y)

    def along_y(f, r, y, forward):
        if forward:
            return at(f, r, y, 1) - at(f, r, y), at(f, r, y, 2) - at(f, r, y, -1)
        return at(f, r, y) - at(f, r, y, -1), at(f, r, y, 1) - at(f, r, y, -2)

    def along_z(f, r, y, forward):
        here = at(f, r, y)

        def moved(k):
            turned = pltpu.roll(here, (-k) % NZ, 1)
            return jnp.where(wide < NZ - k if k > 0 else wide >= -k, turned, 0.0)

        if forward:
            return moved(1) - here, moved(2) - moved(-1)
        return here - moved(-1), moved(1) - moved(-2)

    def total(*parts):
        near, far = parts[0]
        for more in parts[1:]:
            near, far = near + more[0], far + more[1]
        return 27.0 * near - far

    def mask_of(t, y):
        return jnp.tile(masks[t, y // BLK], (BLK // 8, 1))

    def keep(t, r, y, mask):
        return 1.0 + mask * model[QUA, r, y:y + BLK, :]

    def put(f, r, y, value):
        fields[f, LO + r, PAD + y:PAD + y + BLK, :] = value

    def begin(t, f, coefficient, gradient):
        for r, y in tiles:
            mask = mask_of(t, y)
            factor = mask * model[coefficient, r, y:y + BLK, :]
            put(f, r, y, keep(t, r, y, mask) * at(f, r, y) + factor * gradient(r, y))

    def finish(t, f, coefficient, gradient):
        for r, y in tiles:
            factor = mask_of(t, y) * model[coefficient, r, y:y + BLK, :]
            put(f, r, y, at(f, r, y) + factor * gradient(r, y))

    def begin_normal(t):
        for r, y in tiles:
            mask = mask_of(t, y)
            kept = keep(t, r, y, mask)
            shear = mask * model[MU, r, y:y + BLK, :]
            twice = shear + shear
            second, third = total(along_y(VY, r, y, False)), total(along_z(VZ, r, y, False))
            swell = mask * model[LAM, r, y:y + BLK, :] * (second + third)
            put(SXX, r, y, kept * at(SXX, r, y) + swell)
            put(SYY, r, y, kept * at(SYY, r, y) + (swell + twice * second))
            put(SZZ, r, y, kept * at(SZZ, r, y) + (swell + twice * third))

    def finish_normal(t):
        for r, y in tiles:
            mask = mask_of(t, y)
            first = mask * total(along_x(VX, r, y, False))
            shear = model[MU, r, y:y + BLK, :]
            swell = model[LAM, r, y:y + BLK, :] * first
            put(SXX, r, y, at(SXX, r, y) + (swell + (shear + shear) * first))
            put(SYY, r, y, at(SYY, r, y) + swell)
            put(SZZ, r, y, at(SZZ, r, y) + swell)

    for copy in loads:
        copy.wait()

    stores = [pltpu.make_async_copy(inside(f, pl.ds(LO, ROWS)), out.at[f], out_sem.at[f]) for f in range(9)]

    def body(t, carry):
        again = t < STEPS - 1

        def store(*some):
            @pl.when(t == STEPS - 1)
            def _():
                for f in some:
                    stores[f].start()

        def reuse(f):
            @pl.when(t > 0)
            def _():
                sent(f)

        reuse(VX)
        begin(t, VX, BUO, lambda r, y: total(along_y(SXY, r, y, False), along_z(SXZ, r, y, False)))
        reuse(VY)
        begin(t, VY, BUO, lambda r, y: total(along_y(SYY, r, y, True), along_z(SYZ, r, y, False)))
        reuse(VZ)
        begin(t, VZ, BUO, lambda r, y: total(along_y(SYZ, r, y, False), along_z(SZZ, r, y, True)))
        forward(t, *FORWARD[0])
        arrived(SXX)
        finish(t, VX, BUO, lambda r, y: total(along_x(SXX, r, y, True)))
        send(VX, t)
        store(VX)
        forward(t, *FORWARD[1])
        arrived(SXY)
        finish(t, VY, BUO, lambda r, y: total(along_x(SXY, r, y, False)))
        send(VY, t)
        store(VY)

        forward(t, *FORWARD[2])
        arrived(SXZ)
        finish(t, VZ, BUO, lambda r, y: total(along_x(SXZ, r, y, False)))
        send(VZ, t)
        store(VZ)

        @pl.when(t == 0)
        def _():
            pass_on(LAM)
            pass_on(MU)
            gathered(LAM)
            gathered(MU)
            for r, y in tiles:
                spot = (r, slice(y, y + BLK), slice(None))
                factor = (TIME_STEP / 24.0) * (model[(QUA, *spot)] + 1.0)
                model[(LAM, *spot)] = factor * model[(LAM, *spot)]
                model[(MU, *spot)] = factor * model[(MU, *spot)]

        sent(SXX)
        begin_normal(t)
        sent(SXY)
        begin(t, SXY, MU, lambda r, y: total(along_y(VX, r, y, True)))
        sent(SXZ)
        begin(t, SXZ, MU, lambda r, y: total(along_z(VX, r, y, True)))
        begin(t, SYZ, MU, lambda r, y: total(along_z(VY, r, y, True), along_y(VZ, r, y, True)))
        forward(t, *FORWARD[3])
        arrived(VX)
        finish_normal(t)

        @pl.when(again)
        def _():
            send(SXX, t + 1)

        store(SXX, SYY, SZZ, SYZ)

        forward(t, *FORWARD[4])
        arrived(VY)
        finish(t, SXY, MU, lambda r, y: total(along_x(VY, r, y, True)))

        @pl.when(again)
        def _():
            send(SXY, t + 1)

        store(SXY)

        forward(t, *FORWARD[5])
        arrived(VZ)
        finish(t, SXZ, MU, lambda r, y: total(along_x(VZ, r, y, True)))

        @pl.when(again)
        def _():
            send(SXZ, t + 1)

        store(SXZ)

        return carry

    lax.fori_loop(0, STEPS, body, 0)

    for f in (VX, VY, VZ):
        sent(f)
    for role in roles:
        @pl.when(role[0])
        def _():
            for f in LAYERS:
                onward(f, role).wait_send()

    for f in range(4):
        for hop in range(2):
            share(f, hop).wait_send()
    for copy in stores:
        copy.wait()


def solution(mesh):
    n_aper, n_shot = mesh.shape["aper"], mesh.shape["shot"]

    def per_device(wavefield, lame_lambda, lame_mu, buoyancy, quality, active):
        hbm = pl.BlockSpec(memory_space=pltpu.HBM)
        result = pl.pallas_call(
            functools.partial(kernel, n_aper, n_shot),
            out_shape=jax.ShapeDtypeStruct((9, ROWS, NY, NZ), jnp.float32),
            in_specs=[hbm] * 6,
            out_specs=pl.BlockSpec(memory_space=pl.ANY),
            scratch_shapes=[
                pltpu.VMEM((9, ROWS + 2 * LO, NY + 2 * PAD, NZ), jnp.float32),
                pltpu.VMEM((4, ROWS, NY, NZ), jnp.float32),
                pltpu.VMEM((STEPS, NY // BLK, 8, NZ), jnp.float32),
                pltpu.SMEM((STEPS, NY // BLK, NZ // BLK, n_aper), jnp.int32),
                pltpu.SemaphoreType.DMA((9,)),
                pltpu.SemaphoreType.DMA,
                pltpu.SemaphoreType.DMA((4,)),
                pltpu.SemaphoreType.DMA((4, 3)),
                pltpu.SemaphoreType.DMA((4, 3)),
                pltpu.SemaphoreType.DMA((9, 2)),
                pltpu.SemaphoreType.DMA((9, 2, 3)),
                pltpu.SemaphoreType.DMA((9,)),
                pltpu.VMEM((STEPS, 2, 9, LO, max(PIECES[1:]), NZ), jnp.float32),
                pltpu.SemaphoreType.DMA((9, 2)),
                pltpu.SemaphoreType.DMA((9, 2)),
                pltpu.SemaphoreType.DMA((9, 2)),
            ],
            compiler_params=pltpu.CompilerParams(
                collective_id=0, has_side_effects=True, vmem_limit_bytes=32 * 2**20
            ),
            name="elastic_steps",
        )(*(pltpu.with_memory_space_constraint(x, pltpu.HBM) for x in (wavefield[0], lame_lambda, lame_mu, buoyancy, quality, jnp.transpose(active, (0, 2, 3, 1)))))
        return result[None]

    return jax.shard_map(
        per_device,
        mesh=mesh,
        in_specs=(
            P("shot", None, "aper", None, None),
            P("aper", "shot", None),
            P("aper", "shot", None),
            P("aper", "shot", None),
            P("aper", "shot", None),
            P(),
        ),
        out_specs=P("shot", None, "aper", None, None),
        check_vma=False,
    )
```

```python
import functools

import jax
import jax.numpy as jnp
from jax import lax
from jax.experimental import pallas as pl
from jax.experimental.pallas import tpu as pltpu
from jax.sharding import PartitionSpec as P

BLK = 32
STEPS = 4
TIME_STEP = 0.2
MESH = pl.DeviceIdType.MESH

VX, VY, VZ, SXX, SYY, SZZ, SXY, SXZ, SYZ = range(9)
LAM, MU, BUO, QUA = range(4)
ROWS = 4
NY = 128
NZ = 128
PAD = 8
LO = 2

PLANE = 16
SIDE = 4
PIECES = (56, 32, 40)

FIRST = 0
FORWARD = ((SXX,), (SXY,), (SXZ,), (VX,), (VY,), (VZ,))

LAYERS = {SXX: (1, 2), SXY: (2, 1), SXZ: (2, 1), VX: (2, 1), VY: (1, 2), VZ: (1, 2)}


def kernel(n_aper, n_shot, w, lam, mu, buo, qua, act, out, fields, model, masks, blocks, load_sem, act_sem, own_sem,
           gather_send, gather_recv, halo_send, halo_recv, out_sem, relay, leg_send, leg_recv, onward_send):
    me = lax.axis_index("aper")
    shot = lax.axis_index("shot")
    has_up = me < n_aper - 1
    has_down = me > 0
    up = jnp.minimum(me + 1, n_aper - 1)
    down = jnp.maximum(me - 1, 0)
    width = NY // n_shot
    shards = (lam, mu, buo, qua)

    def inside(f, rows):
        return fields.at[f, rows, PAD:PAD + NY, :]

    local = lax.rem(me, PLANE)
    last_plane = me >= n_aper - PLANE
    first_plane = me < PLANE
    crosses_up = jnp.logical_and(local == PLANE - 1, jnp.logical_not(last_plane))
    crosses_down = jnp.logical_and(local == 0, jnp.logical_not(first_plane))
    plain_up = jnp.logical_and(has_up, jnp.logical_not(crosses_up))
    plain_down = jnp.logical_and(has_down, jnp.logical_not(crosses_down))
    not_last, not_first = jnp.logical_not(last_plane), jnp.logical_not(first_plane)
    roles = [
        (jnp.logical_and(local == PLANE - SIDE, not_last), SIDE - 1, SIDE, True, 1),
        (jnp.logical_and(local == SIDE - 1, not_last), PLANE - SIDE, PLANE - SIDE + 1, True, 2),
        (jnp.logical_and(local == SIDE - 1, not_first), 1 - SIDE, -SIDE, False, 1),
        (jnp.logical_and(local == PLANE - SIDE, not_first), SIDE - PLANE, SIDE - PLANE - 1, False, 2),
    ]
    starts = [sum(PIECES[:k]) for k in range(len(PIECES))]

    def clipped(index):
        return jnp.clip(index, 0, n_aper - 1)

    def span(k):
        return pl.ds(PAD + starts[k], PIECES[k])

    def edge(f, to_up):
        count = LAYERS[f][0 if to_up else 1]
        if to_up:
            return pl.ds(LO + ROWS - count, count), pl.ds(LO - count, count)
        return pl.ds(LO, count), pl.ds(LO + ROWS, count)

    def leaving(f, to_up, ys, source):
        rows = edge(f, to_up)[0]
        if source is None:
            return fields.at[f, rows, ys, :]
        return source.at[f, pl.ds(rows.start - LO, rows.size), pl.ds(ys.start - PAD, ys.size), :]

    def halo(f, to_up, k=None, source=None):
        ys = pl.ds(PAD, NY) if k is None else span(k)
        side = 0 if to_up else 1
        return pltpu.make_async_remote_copy(
            src_ref=leaving(f, to_up, ys, source), dst_ref=fields.at[f, edge(f, to_up)[1], ys, :],
            send_sem=halo_send.at[f, side], recv_sem=halo_recv.at[f, side, k or 0],
            device_id=(up if to_up else down, shot), device_id_type=MESH)

    def leg(f, to_up, k, source=None, t=0):
        away = SIDE - 1 if k == 1 else PLANE - SIDE
        target = me - away if to_up else me + away
        return pltpu.make_async_remote_copy(
            src_ref=leaving(f, to_up, span(k), source),
            dst_ref=relay.at[t, 0 if to_up else 1, f, pl.ds(0, edge(f, to_up)[0].size), pl.ds(0, PIECES[k]), :],
            send_sem=leg_send.at[f, k - 1], recv_sem=leg_recv.at[f, 0 if to_up else 1], device_id=(clipped(target), shot), device_id_type=MESH)

    def onward(f, role, t=0):
        _, _, offset, to_up, k = role
        rows, side = edge(f, to_up)[1], 0 if to_up else 1
        return pltpu.make_async_remote_copy(
            src_ref=relay.at[t, side, f, pl.ds(0, rows.size), pl.ds(0, PIECES[k]), :], dst_ref=fields.at[f, rows, span(k), :],
            send_sem=onward_send.at[f, side], recv_sem=halo_recv.at[f, side, k],
            device_id=(clipped(me + offset), shot), device_id_type=MESH)

    def send(f, t, source=None):
        for to_up, crosses, plain in ((True, crosses_up, plain_up), (False, crosses_down, plain_down)):
            @pl.when(crosses)
            def _():
                leg(f, to_up, 1, source, t).start()
                leg(f, to_up, 2, source, t).start()
                halo(f, to_up, 0, source).start()

            @pl.when(plain)
            def _():
                halo(f, to_up, None, source).start()

    def sent(f):
        for to_up, crosses, plain in ((True, crosses_up, plain_up), (False, crosses_down, plain_down)):
            @pl.when(crosses)
            def _():
                leg(f, to_up, 1).wait_send()
                leg(f, to_up, 2).wait_send()
                halo(f, to_up, 0).wait_send()

            @pl.when(plain)
            def _():
                halo(f, to_up).wait_send()

    def arrived(f):
        for to_up, crosses, plain in ((True, crosses_down, plain_down), (False, crosses_up, plain_up)):
            @pl.when(crosses)
            def _():
                for k in range(len(PIECES)):
                    halo(f, to_up, k).wait_recv()

            @pl.when(plain)
            def _():
                halo(f, to_up).wait_recv()

    def relayed(t, *some):
        for f in some:
            for role in roles:
                @pl.when(role[0])
                def _():
                    if t is not FIRST:
                        @pl.when(t > 0)
                        def _():
                            onward(f, role).wait_send()

                    leg(f, role[3], role[4]).wait_recv()
                    onward(f, role, t).start()

    def forward(t, *some):
        now = [f for f in some if f in (VX, VY, VZ)]
        if now:
            relayed(t, *now)
        later = [f for f in some if f not in now]
        if later:
            @pl.when(t > 0)
            def _():
                relayed(t, *later)

    partner = shot + 1 - 2 * lax.rem(shot, 2)
    across = lax.rem(shot + 2, n_shot)

    def shard_rows(owner):
        return pl.ds(pl.multiple_of(owner * width, width), width)

    def share(f, hop):
        place = model.at[f, :, shard_rows(across if hop == 2 else shot), :]
        return pltpu.make_async_remote_copy(
            src_ref=place if hop == 2 else shards[f], dst_ref=place, send_sem=gather_send.at[f, hop],
            recv_sem=gather_recv.at[f, hop], device_id=(me, across if hop == 1 else partner), device_id_type=MESH)

    def pass_on(f):
        share(f, 1).wait_recv()
        share(f, 2).start()

    loads = [pltpu.make_async_copy(w.at[f], inside(f, pl.ds(LO, ROWS)), load_sem.at[f]) for f in range(9)]
    own = [pltpu.make_async_copy(shards[f], model.at[f, :, shard_rows(shot), :], own_sem.at[f]) for f in range(4)]
    flags = pltpu.make_async_copy(act, blocks, act_sem)

    barrier = pltpu.get_barrier_semaphore()

    greeted = [(has_up, me + 1), (has_down, me - 1)]
    for crossing, sign in ((crosses_up, 1), (crosses_down, -1)):
        greeted += [(crossing, me - sign * (SIDE - 1)), (crossing, me - sign * (PLANE - SIDE)),
                    (crossing, me + sign * SIDE), (crossing, me + sign * (PLANE - SIDE + 1))]
    for here, origin, target, _, _ in roles:
        greeted += [(here, me + origin), (here, me + target)]
    for here, whom in greeted:
        @pl.when(here)
        def _():
            pl.semaphore_signal(barrier, inc=1, device_id=(clipped(whom), shot), device_id_type=MESH)

    for peer in (partner, across):
        pl.semaphore_signal(barrier, inc=1, device_id=(me, peer), device_id_type=MESH)

    flags.start()
    for copy in loads + own:
        copy.start()

    zeros = jnp.zeros((ROWS, PAD, NZ), jnp.float32)
    for f in range(9):
        fields[f, LO:LO + ROWS, 0:PAD, :] = zeros
        fields[f, LO:LO + ROWS, PAD + NY:, :] = zeros

    @pl.when(jnp.logical_not(has_down))
    def _():
        for f in LAYERS:
            fields[f, 0:LO, PAD:PAD + NY, :] = jnp.zeros((LO, NY, NZ), jnp.float32)

    @pl.when(jnp.logical_not(has_up))
    def _():
        for f in LAYERS:
            fields[f, LO + ROWS:, PAD:PAD + NY, :] = jnp.zeros((LO, NY, NZ), jnp.float32)

    pl.semaphore_wait(barrier, 2 + sum(here.astype(jnp.int32) for here, _ in greeted))

    for f in (QUA, BUO):
        for hop in (1, 0):
            share(f, hop).start()
    for f in (SXX, SXY, SXZ):
        send(f, 0, w)

    lane = lax.broadcasted_iota(jnp.int32, (8, NZ), 1)
    flags.wait()
    for t in range(STEPS):
        for b in range(NY // BLK):
            on = [blocks[t, b, k, me].astype(jnp.float32) for k in range(NZ // BLK)]
            masks[t, b] = jnp.where(lane < BLK, on[0], jnp.where(lane < 2 * BLK, on[1],
                                    jnp.where(lane < 3 * BLK, on[2], on[3])))

    relayed(FIRST, SXX, SXY, SXZ)

    def gathered(f):
        own[f].wait()
        for hop in (0, 2):
            share(f, hop).wait_recv()
        share(f, 2).wait_send()

    tiles = [(r, b * BLK) for b in range(NY // BLK) for r in range(ROWS)]

    pass_on(QUA)
    pass_on(BUO)
    gathered(QUA)
    gathered(BUO)
    for f in (LAM, MU):
        for hop in (1, 0):
            share(f, hop).start()
    for r, y in tiles:
        at = (r, slice(y, y + BLK), slice(None))
        damping = jnp.exp(-TIME_STEP * model[(QUA, *at)])
        model[(QUA, *at)] = damping - 1.0
        model[(BUO, *at)] = (TIME_STEP / 24.0) * damping * model[(BUO, *at)]

    wide = lax.broadcasted_iota(jnp.int32, (BLK, NZ), 1)

    def at(f, r, y, dy=0):
        return fields[f, LO + r, PAD + y + dy:PAD + y + dy + BLK, :]

    def along_x(f, r, y, forward):
        if forward:
            return at(f, r + 1, y) - at(f, r, y), at(f, r + 2, y) - at(f, r - 1, y)
        return at(f, r, y) - at(f, r - 1, y), at(f, r + 1, y) - at(f, r - 2, y)

    def along_y(f, r, y, forward):
        if forward:
            return at(f, r, y, 1) - at(f, r, y), at(f, r, y, 2) - at(f, r, y, -1)
        return at(f, r, y) - at(f, r, y, -1), at(f, r, y, 1) - at(f, r, y, -2)

    def along_z(f, r, y, forward):
        here = at(f, r, y)

        def moved(k):
            turned = pltpu.roll(here, (-k) % NZ, 1)
            return jnp.where(wide < NZ - k if k > 0 else wide >= -k, turned, 0.0)

        if forward:
            return moved(1) - here, moved(2) - moved(-1)
        return here - moved(-1), moved(1) - moved(-2)

    def total(*parts):
        near, far = parts[0]
        for more in parts[1:]:
            near, far = near + more[0], far + more[1]
        return 27.0 * near - far

    def mask_of(t, y):
        return jnp.tile(masks[t, y // BLK], (BLK // 8, 1))

    def keep(t, r, y, mask):
        return 1.0 + mask * model[QUA, r, y:y + BLK, :]

    def put(f, r, y, value):
        fields[f, LO + r, PAD + y:PAD + y + BLK, :] = value

    def begin(t, f, coefficient, gradient):
        for r, y in tiles:
            mask = mask_of(t, y)
            factor = mask * model[coefficient, r, y:y + BLK, :]
            put(f, r, y, keep(t, r, y, mask) * at(f, r, y) + factor * gradient(r, y))

    def finish(t, f, coefficient, gradient):
        for r, y in tiles:
            factor = mask_of(t, y) * model[coefficient, r, y:y + BLK, :]
            put(f, r, y, at(f, r, y) + factor * gradient(r, y))

    def begin_normal(t):
        for r, y in tiles:
            mask = mask_of(t, y)
            kept = keep(t, r, y, mask)
            shear = mask * model[MU, r, y:y + BLK, :]
            twice = shear + shear
            second, third = total(along_y(VY, r, y, False)), total(along_z(VZ, r, y, False))
            swell = mask * model[LAM, r, y:y + BLK, :] * (second + third)
            put(SXX, r, y, kept * at(SXX, r, y) + swell)
            put(SYY, r, y, kept * at(SYY, r, y) + (swell + twice * second))
            put(SZZ, r, y, kept * at(SZZ, r, y) + (swell + twice * third))

    def finish_normal(t):
        for r, y in tiles:
            mask = mask_of(t, y)
            first = mask * total(along_x(VX, r, y, False))
            shear = model[MU, r, y:y + BLK, :]
            swell = model[LAM, r, y:y + BLK, :] * first
            put(SXX, r, y, at(SXX, r, y) + (swell + (shear + shear) * first))
            put(SYY, r, y, at(SYY, r, y) + swell)
            put(SZZ, r, y, at(SZZ, r, y) + swell)

    for copy in loads:
        copy.wait()

    stores = [pltpu.make_async_copy(inside(f, pl.ds(LO, ROWS)), out.at[f], out_sem.at[f]) for f in range(9)]

    def body(t, carry):
        again = t < STEPS - 1

        def store(*some):
            @pl.when(t == STEPS - 1)
            def _():
                for f in some:
                    stores[f].start()

        def reuse(f):
            @pl.when(t > 0)
            def _():
                sent(f)

        reuse(VX)
        begin(t, VX, BUO, lambda r, y: total(along_y(SXY, r, y, False), along_z(SXZ, r, y, False)))
        reuse(VY)
        begin(t, VY, BUO, lambda r, y: total(along_y(SYY, r, y, True), along_z(SYZ, r, y, False)))
        reuse(VZ)
        begin(t, VZ, BUO, lambda r, y: total(along_y(SYZ, r, y, False), along_z(SZZ, r, y, True)))
        forward(t, *FORWARD[0])
        arrived(SXX)
        finish(t, VX, BUO, lambda r, y: total(along_x(SXX, r, y, True)))
        send(VX, t)
        store(VX)
        forward(t, *FORWARD[1])
        arrived(SXY)
        finish(t, VY, BUO, lambda r, y: total(along_x(SXY, r, y, False)))
        send(VY, t)
        store(VY)

        forward(t, *FORWARD[2])
        arrived(SXZ)
        finish(t, VZ, BUO, lambda r, y: total(along_x(SXZ, r, y, False)))
        send(VZ, t)
        store(VZ)

        @pl.when(t == 0)
        def _():
            pass_on(LAM)
            pass_on(MU)
            gathered(LAM)
            gathered(MU)
            for r, y in tiles:
                spot = (r, slice(y, y + BLK), slice(None))
                factor = (TIME_STEP / 24.0) * (model[(QUA, *spot)] + 1.0)
                model[(LAM, *spot)] = factor * model[(LAM, *spot)]
                model[(MU, *spot)] = factor * model[(MU, *spot)]

        sent(SXX)
        begin_normal(t)
        sent(SXY)
        begin(t, SXY, MU, lambda r, y: total(along_y(VX, r, y, True)))
        sent(SXZ)
        begin(t, SXZ, MU, lambda r, y: total(along_z(VX, r, y, True)))
        begin(t, SYZ, MU, lambda r, y: total(along_z(VY, r, y, True), along_y(VZ, r, y, True)))
        forward(t, *FORWARD[3])
        arrived(VX)
        finish_normal(t)

        @pl.when(again)
        def _():
            send(SXX, t + 1)

        store(SXX, SYY, SZZ, SYZ)

        forward(t, *FORWARD[4])
        arrived(VY)
        finish(t, SXY, MU, lambda r, y: total(along_x(VY, r, y, True)))

        @pl.when(again)
        def _():
            send(SXY, t + 1)

        store(SXY)

        forward(t, *FORWARD[5])
        arrived(VZ)
        finish(t, SXZ, MU, lambda r, y: total(along_x(VZ, r, y, True)))

        @pl.when(again)
        def _():
            send(SXZ, t + 1)

        store(SXZ)

        return carry

    lax.fori_loop(0, STEPS, body, 0)

    for f in (VX, VY, VZ):
        sent(f)
    for role in roles:
        @pl.when(role[0])
        def _():
            for f in LAYERS:
                onward(f, role).wait_send()

    for f in range(4):
        for hop in range(2):
            share(f, hop).wait_send()
    for copy in stores:
        copy.wait()


def solution(mesh):
    n_aper, n_shot = mesh.shape["aper"], mesh.shape["shot"]

    def per_device(wavefield, lame_lambda, lame_mu, buoyancy, quality, active):
        hbm = pl.BlockSpec(memory_space=pltpu.HBM)
        result = pl.pallas_call(
            functools.partial(kernel, n_aper, n_shot),
            out_shape=jax.ShapeDtypeStruct((9, ROWS, NY, NZ), jnp.float32),
            in_specs=[hbm] * 6,
            out_specs=pl.BlockSpec(memory_space=pl.ANY),
            scratch_shapes=[
                pltpu.VMEM((9, ROWS + 2 * LO, NY + 2 * PAD, NZ), jnp.float32),
                pltpu.VMEM((4, ROWS, NY, NZ), jnp.float32),
                pltpu.VMEM((STEPS, NY // BLK, 8, NZ), jnp.float32),
                pltpu.SMEM((STEPS, NY // BLK, NZ // BLK, n_aper), jnp.int32),
                pltpu.SemaphoreType.DMA((9,)),
                pltpu.SemaphoreType.DMA,
                pltpu.SemaphoreType.DMA((4,)),
                pltpu.SemaphoreType.DMA((4, 3)),
                pltpu.SemaphoreType.DMA((4, 3)),
                pltpu.SemaphoreType.DMA((9, 2)),
                pltpu.SemaphoreType.DMA((9, 2, 3)),
                pltpu.SemaphoreType.DMA((9,)),
                pltpu.VMEM((STEPS, 2, 9, LO, max(PIECES[1:]), NZ), jnp.float32),
                pltpu.SemaphoreType.DMA((9, 2)),
                pltpu.SemaphoreType.DMA((9, 2)),
                pltpu.SemaphoreType.DMA((9, 2)),
            ],
            compiler_params=pltpu.CompilerParams(
                collective_id=0, has_side_effects=True, vmem_limit_bytes=32 * 2**20
            ),
            name="elastic_steps",
        )(*(pltpu.with_memory_space_constraint(x, pltpu.HBM) for x in (wavefield[0], lame_lambda, lame_mu, buoyancy, quality, jnp.transpose(active, (0, 2, 3, 1)))))
        return result[None]

    return jax.shard_map(
        per_device,
        mesh=mesh,
        in_specs=(
            P("shot", None, "aper", None, None),
            P("aper", "shot", None),
            P("aper", "shot", None),
            P("aper", "shot", None),
            P("aper", "shot", None),
            P(),
        ),
        out_specs=P("shot", None, "aper", None, None),
        check_vma=False,
    )
```
